32 devices in a mesh: row: 4 (over x, core), col: 8 (over z, y).
Axes of the slice: x: 2, y: 2, z: 4, core: 2. Of those that a mesh axis runs over, the one named last changes fastest.
Arguments:
- factor: float32 [8, 8, 2048, 2048], P(None, None, 'row', 'col'), may hold values from -0.046875 to 0.046875
- inverses: float32 [8, 2048, 2048], P(None, 'col', 'row'), may hold values from -1 to 1
- right_side: float32 [128, 8, 2048], P(None, None, 'row'), may hold values from -6 to 6
Outputs:
- forward_solution: float32 [128, 8, 2048], P(None, None, 'col')
- solution: float32 [128, 8, 2048], P(None, None, 'row')
The draws below stay inside these ranges and needn't reach their ends.
All inputs are finite; a program needn't handle non-finite values.
Results may differ from the reference program's by a relative error of at most 0.00012.
Values sent between devices are 32-bit elements; how exact they have to be, the bound alone decides.
A program may use at most 128 MiB of HBM per device.

```python
import math
import jax
import jax.numpy as jnp
from jax import lax

ORDER = 16384
BLOCK = 2048
SIDES = 128
BLOCKS = 8


def draw_inverses(key, part):
    key_diagonal, key_lower = jax.random.split(jax.random.fold_in(key, 11))
    diagonal_values = jax.random.uniform(key_diagonal, (BLOCKS, BLOCK), jnp.float32, 0.5, 1.0)
    lower_part = jax.random.truncated_normal(key_lower, -4.0, 4.0, (BLOCKS, BLOCK, BLOCK), jnp.float32)
    lower_part = lower_part * (0.4 / math.sqrt(BLOCK))
    row_numbers = lax.broadcasted_iota(jnp.int32, (BLOCK, BLOCK), 0)
    col_numbers = lax.broadcasted_iota(jnp.int32, (BLOCK, BLOCK), 1)
    strict = (row_numbers > col_numbers).astype(jnp.float32)
    unit_diagonal = (row_numbers == col_numbers).astype(jnp.float32)
    return lower_part * strict[None] + diagonal_values[:, :, None] * unit_diagonal[None]


def steps_of(key, shape, pieces, low, top_value):
    def one(axis_at, blocks):
        draws = jax.random.uniform(jax.random.fold_in(jax.random.fold_in(key, 6), axis_at), (blocks,), jnp.float32, low / len(pieces), top_value / len(pieces))
        return jnp.repeat(jnp.exp(draws), shape[axis_at] // blocks).reshape((-1,) + (1,) * (len(shape) - axis_at - 1))

    gain = one(*pieces[0])
    for cut in pieces[1:]:
        gain = gain * one(*cut)
    return gain


def scatter_about(rng, shape, scale, limit, pieces=(), kind=jnp.bfloat16):
    entries = scale * jax.random.normal(rng, shape, jnp.float32)
    if pieces:
        entries = entries * steps_of(rng, shape, pieces, -0.22, 0.18)
    return jnp.clip(entries, -limit, limit).astype(kind)


def setup_inputs(seed: int = 0) -> dict:
    arg_keys = jax.random.split(jax.random.key(seed), 4)
    return {
        "factor": scatter_about(arg_keys[0], (BLOCKS, BLOCKS, BLOCK, BLOCK), ORDER ** -0.5, 0.046875, ((2, 4), (3, 8)), jnp.float32),
        "inverses": draw_inverses(jax.random.fold_in(arg_keys[3], 71), 0),
        "right_side": scatter_about(arg_keys[2], (SIDES, BLOCKS, BLOCK), 1.0, 6.0, ((2, 4),), jnp.float32),
    }


def reference(factor, inverses, right_side):
    highest = lax.Precision.HIGHEST
    forward = []
    for number in range(BLOCKS):
        target = right_side[:, number]
        if number > 0:
            earlier = jnp.stack(forward, 1)
            target = target - jnp.einsum("sjb,jdb->sd", earlier, factor[number, :number], precision=highest)
        forward.append(jnp.dot(target, inverses[number].T, precision=highest))
    backward = [None] * BLOCKS
    for number in range(BLOCKS - 1, -1, -1):
        target = forward[number]
        if number < BLOCKS - 1:
            later = jnp.stack(backward[number + 1:], 1)
            target = target - jnp.einsum("sid,idb->sb", later, factor[number + 1:, number], precision=highest)
        backward[number] = jnp.dot(target, inverses[number], precision=highest)
    return (jnp.stack(forward, 1), jnp.stack(backward, 1))
```

```python
import functools

import jax
import jax.numpy as jnp
from jax import lax
from jax.experimental import pallas as pl
from jax.experimental.pallas import tpu as pltpu
from jax.sharding import PartitionSpec as P

MESH = pl.DeviceIdType.MESH
NN = (((1,), (0,)), ((), ()))
NT = (((1,), (1,)), ((), ()))


def split(value):
    high = value.astype(jnp.bfloat16)
    low = (value - high.astype(jnp.float32)).astype(jnp.bfloat16)
    return high, low


def product(left, right, dims):
    count = left.shape[0]
    left_high, left_low = split(left)
    right_high, right_low = split(right)
    both = lax.dot_general(
        jnp.concatenate([left_high, left_low], 0), right_high, dims, preferred_element_type=jnp.float32
    )
    rest = lax.dot_general(left_high, right_low, dims, preferred_element_type=jnp.float32)
    return both[:count] + (both[count:] + rest)


def kernel(
    rows, cols, groups,
    factor_hbm, inverses_hbm, right_ref,
    forward_ref, backward_ref,
    factor, inverses, ahead, behind, target_row, target_col, part_col, part_row, in_row, in_col,
    factor_sem, inverse_sem,
    rs_row_send, rs_row_recv, ag_row_send, ag_row_recv,
    rs_col_send, rs_col_recv, ag_col_send, ag_col_recv,
):
    blocks = right_ref.shape[0]
    row_width = right_ref.shape[-1]
    col_width = forward_ref.shape[-1]
    row_sides, col_sides = forward_ref.shape[3], right_ref.shape[3]
    sides = rows * row_sides
    row_me, col_me = lax.axis_index("row"), lax.axis_index("col")

    def fetch_factor(i, j):
        return pltpu.make_async_copy(factor_hbm.at[i, j], factor.at[i, j], factor_sem.at[i, j])

    def fetch_inverse(k):
        return pltpu.make_async_copy(inverses_hbm.at[k], inverses.at[k], inverse_sem.at[k])

    for k in range(blocks):
        fetch_inverse(k).start()
        for i in range(k + 1, blocks):
            fetch_factor(i, k).start()

    barrier = pltpu.get_barrier_semaphore()
    for axis, size, me in (("row", rows, row_me), ("col", cols, col_me)):
        for offset in range(1, size):
            pl.semaphore_signal(
                barrier, inc=1, device_id={axis: lax.rem(me + offset, size)}, device_id_type=MESH
            )
    ahead[...] = jnp.zeros_like(ahead)
    behind[...] = jnp.zeros_like(behind)
    pl.semaphore_wait(barrier, rows + cols - 2)

    def scatter(axis, size, me, source, landing, send, recv, g):
        out = []
        for offset in range(1, size):
            peer = lax.rem(me + offset, size)
            out.append(pltpu.make_async_remote_copy(
                src_ref=source.at[peer], dst_ref=landing.at[g, offset],
                send_sem=send.at[g, offset], recv_sem=recv.at[g, offset],
                device_id={axis: peer}, device_id_type=MESH,
            ))
        return out

    def gather(axis, size, me, buffer, send, recv, g):
        out = []
        for offset in range(1, size):
            peer = lax.rem(me + offset, size)
            out.append(pltpu.make_async_remote_copy(
                src_ref=buffer.at[me], dst_ref=buffer.at[me],
                send_sem=send.at[g, offset], recv_sem=recv.at[g, offset],
                device_id={axis: peer}, device_id_type=MESH,
            ))
        return out

    def scatter_row(source, g):
        return scatter("row", rows, row_me, source, in_row, rs_row_send, rs_row_recv, g)

    def scatter_col(source, g):
        return scatter("col", cols, col_me, source, in_col, rs_col_send, rs_col_recv, g)

    def gather_row(buffer, g):
        return gather("row", rows, row_me, buffer, ag_row_send, ag_row_recv, g)

    def gather_col(buffer, g):
        return gather("col", cols, col_me, buffer, ag_col_send, ag_col_recv, g)

    def start(copies):
        for copy in copies:
            copy.start()

    def finish(copies):
        for copy in copies:
            copy.wait_recv()
        for copy in copies:
            copy.wait_send()

    def reduced(mine, landing, g, size):
        total = mine
        for offset in range(1, size):
            total = total + landing[g, offset]
        return total

    def flat(value):
        return value.reshape(sides, value.shape[-1])

    def by_row(value):
        return value.reshape(rows, row_sides, value.shape[-1])

    def by_col(value):
        return value.reshape(cols, col_sides, value.shape[-1])

    def everything(ref, k):
        return ref[k].reshape(groups * sides, ref.shape[-1])

    def finish_forward(k):
        for g in range(groups):
            finish(scatter_row(part_row.at[g], g))
            forward_ref[k, g, row_me] = reduced(part_row[g, row_me], in_row, g, rows)
            start(gather_row(forward_ref.at[k, g], g))

    fetch_inverse(0).wait()
    for g in range(groups):
        part_row[g] = by_row(product(flat(right_ref[0, g]), inverses[0], NT))
        start(scatter_row(part_row.at[g], g))
    finish_forward(0)

    def forward_step(k, _):
        fetch_factor(k, k - 1).wait()
        for g in range(groups):
            finish(gather_row(forward_ref.at[k - 1, g], g))
            ahead[k, g] += by_col(product(flat(forward_ref[k - 1, g]), factor[k, k - 1], NT))
            start(scatter_col(ahead.at[k, g], g))

        def update(i, _):
            fetch_factor(i, k - 1).wait()
            ahead[i] += product(everything(forward_ref, k - 1), factor[i, k - 1], NT).reshape(ahead.shape[1:])
            return 0

        lax.fori_loop(k + 1, blocks, update, 0)
        fetch_inverse(k).wait()
        for g in range(groups):
            finish(scatter_col(ahead.at[k, g], g))
            total = reduced(ahead[k, g, col_me], in_col, g, cols)
            target_row[g, col_me] = right_ref[k, g, col_me] - total
            start(gather_col(target_row.at[g], g))
        for g in range(groups):
            finish(gather_col(target_row.at[g], g))
            part_row[g] = by_row(product(flat(target_row[g]), inverses[k], NT))
            start(scatter_row(part_row.at[g], g))
        finish_forward(k)
        return 0

    lax.fori_loop(1, blocks, forward_step, 0)

    def finish_backward(k):
        for g in range(groups):
            finish(scatter_col(part_col.at[g], g))
            backward_ref[k, g, col_me] = reduced(part_col[g, col_me], in_col, g, cols)
            start(gather_col(backward_ref.at[k, g], g))

    last = blocks - 1
    for g in range(groups):
        finish(gather_row(forward_ref.at[last, g], g))
        part_col[g] = by_col(product(flat(forward_ref[last, g]), inverses[last], NN))
        start(scatter_col(part_col.at[g], g))
    finish_backward(last)

    def backward_step(step, _):
        k = last - step
        for g in range(groups):
            finish(gather_col(backward_ref.at[k + 1, g], g))
            behind[k, g] += by_row(product(flat(backward_ref[k + 1, g]), factor[k + 1, k], NN))
            start(scatter_row(behind.at[k, g], g))

        def update(j, _):
            behind[j] += product(everything(backward_ref, k + 1), factor[k + 1, j], NN).reshape(behind.shape[1:])
            return 0

        lax.fori_loop(0, k, update, 0)
        for g in range(groups):
            finish(scatter_row(behind.at[k, g], g))
            total = reduced(behind[k, g, row_me], in_row, g, rows)
            target_col[g, row_me] = forward_ref[k, g, row_me] - total
            start(gather_row(target_col.at[g], g))
        for g in range(groups):
            finish(gather_row(target_col.at[g], g))
            part_col[g] = by_col(product(flat(target_col[g]), inverses[k], NN))
            start(scatter_col(part_col.at[g], g))
        finish_backward(k)
        return 0

    lax.fori_loop(1, blocks, backward_step, 0)
    for g in range(groups):
        finish(gather_col(backward_ref.at[0, g], g))


def local(rows, cols, factor, inverses, right_side):
    blocks, _, row_width, col_width = factor.shape
    sides = right_side.shape[0]
    groups = 2 if sides % (16 * rows) == 0 and sides % (16 * cols) == 0 else 1
    row_sides, col_sides = sides // (groups * rows), sides // (groups * cols)
    wide = (groups, cols, col_sides, row_width)
    narrow = (groups, rows, row_sides, col_width)
    right = right_side.transpose(1, 0, 2).reshape((blocks,) + wide)
    f32 = jnp.float32
    vmem = pl.BlockSpec(memory_space=pltpu.VMEM)
    hbm = pl.BlockSpec(memory_space=pl.ANY)
    dma = pltpu.SemaphoreType.DMA
    forward, backward = pl.pallas_call(
        functools.partial(kernel, rows, cols, groups),
        out_shape=(
            jax.ShapeDtypeStruct((blocks,) + narrow, f32),
            jax.ShapeDtypeStruct((blocks,) + wide, f32),
        ),
        in_specs=[hbm, hbm, vmem],
        out_specs=(vmem, vmem),
        scratch_shapes=[
            pltpu.VMEM(factor.shape, f32),
            pltpu.VMEM(inverses.shape, f32),
            pltpu.VMEM((blocks,) + wide, f32),
            pltpu.VMEM((blocks,) + narrow, f32),
            pltpu.VMEM(wide, f32),
            pltpu.VMEM(narrow, f32),
            pltpu.VMEM(wide, f32),
            pltpu.VMEM(narrow, f32),
            pltpu.VMEM(narrow, f32),
            pltpu.VMEM(wide, f32),
            dma((blocks, blocks)),
            dma((blocks,)),
        ] + [dma((groups, rows))] * 4 + [dma((groups, cols))] * 4,
        compiler_params=pltpu.CompilerParams(
            collective_id=0, has_side_effects=True, vmem_limit_bytes=56 * 1024 * 1024
        ),
    )(factor, inverses, right)
    forward = forward.reshape(blocks, sides, col_width).transpose(1, 0, 2)
    backward = backward.reshape(blocks, sides, row_width).transpose(1, 0, 2)
    return forward, backward


def solution(mesh):
    placed = (P(None, None, "row", "col"), P(None, "col", "row"), P(None, None, "row"))
    return jax.shard_map(
        functools.partial(local, mesh.shape["row"], mesh.shape["col"]),
        mesh=mesh,
        in_specs=placed,
        out_specs=(P(None, None, "col"), P(None, None, "row")),
        check_vma=False,
    )
```

```python
import functools

import jax
import jax.numpy as jnp
from jax import lax
from jax.experimental import pallas as pl
from jax.experimental.pallas import tpu as pltpu
from jax.sharding import PartitionSpec as P

MESH = pl.DeviceIdType.MESH
NN = (((1,), (0,)), ((), ()))
NT = (((1,), (1,)), ((), ()))


def split(value):
    high = value.astype(jnp.bfloat16)
    low = (value - high.astype(jnp.float32)).astype(jnp.bfloat16)
    return high, low


def product(left, right, dims):
    count = left.shape[0]
    left_high, left_low = split(left)
    right_high, right_low = split(right)
    both = lax.dot_general(
        jnp.concatenate([left_high, left_low], 0), right_high, dims, preferred_element_type=jnp.float32
    )
    rest = lax.dot_general(left_high, right_low, dims, preferred_element_type=jnp.float32)
    return both[:count] + (both[count:] + rest)


def kernel(
    rows, cols, groups,
    factor_hbm, inverses_hbm, right_ref,
    forward_ref, backward_ref,
    factor, inverses, ahead, behind, target_row, target_col, part_col, part_row, in_row, in_col,
    factor_sem, inverse_sem,
    rs_row_send, rs_row_recv, ag_row_send, ag_row_recv,
    rs_col_send, rs_col_recv, ag_col_send, ag_col_recv,
):
    blocks = right_ref.shape[0]
    row_width = right_ref.shape[-1]
    col_width = forward_ref.shape[-1]
    row_sides, col_sides = forward_ref.shape[3], right_ref.shape[3]
    sides = rows * row_sides
    row_me, col_me = lax.axis_index("row"), lax.axis_index("col")

    def fetch_factor(i, j):
        return pltpu.make_async_copy(factor_hbm.at[i, j], factor.at[i, j], factor_sem.at[i, j])

    def fetch_inverse(k):
        return pltpu.make_async_copy(inverses_hbm.at[k], inverses.at[k], inverse_sem.at[k])

    for k in range(blocks):
        fetch_inverse(k).start()
        for i in range(k + 1, blocks):
            fetch_factor(i, k).start()

    barrier = pltpu.get_barrier_semaphore()
    for axis, size, me in (("row", rows, row_me), ("col", cols, col_me)):
        for offset in range(1, size):
            pl.semaphore_signal(
                barrier, inc=1, device_id={axis: lax.rem(me + offset, size)}, device_id_type=MESH
            )
    ahead[...] = jnp.zeros_like(ahead)
    behind[...] = jnp.zeros_like(behind)
    pl.semaphore_wait(barrier, rows + cols - 2)

    class Phase:
        def __init__(self, axis, size, me, pairs, counted, send, recv):
            self.axis, self.size, self.me = axis, size, me
            self.pairs, self.counted, self.send, self.recv = pairs, counted, send, recv

        def start(self):
            for offset in range(1, self.size):
                peer = lax.rem(self.me + offset, self.size)
                source, target = self.pairs(peer, offset)
                pltpu.make_async_remote_copy(
                    src_ref=source, dst_ref=target, send_sem=self.send, recv_sem=self.recv,
                    device_id={self.axis: peer}, device_id_type=MESH,
                ).start()

        def arrived(self):
            pltpu.make_async_copy(self.counted, self.counted, self.recv).wait()

        def sent(self):
            pltpu.make_async_copy(self.counted, self.counted, self.send).wait()

    def scatter(axis, size, me, source, landing, send, recv, g):
        return Phase(
            axis, size, me, lambda peer, offset: (source.at[peer], landing.at[g, offset - 1]),
            landing.at[g], send.at[g], recv.at[g],
        )

    def gather(axis, size, me, buffer, send, recv, g):
        return Phase(
            axis, size, me, lambda peer, offset: (buffer.at[me], buffer.at[me]),
            buffer.at[pl.ds(0, size - 1)], send.at[g], recv.at[g],
        )

    def scatter_row(source, g):
        return scatter("row", rows, row_me, source, in_row, rs_row_send, rs_row_recv, g)

    def scatter_col(source, g):
        return scatter("col", cols, col_me, source, in_col, rs_col_send, rs_col_recv, g)

    def gather_row(buffer, g):
        return gather("row", rows, row_me, buffer, ag_row_send, ag_row_recv, g)

    def gather_col(buffer, g):
        return gather("col", cols, col_me, buffer, ag_col_send, ag_col_recv, g)

    def reduced(mine, landing, g, size):
        total = mine
        for slot in range(size - 1):
            total = total + landing[g, slot]
        return total

    def flat(value):
        return value.reshape(sides, value.shape[-1])

    def by_row(value):
        return value.reshape(rows, row_sides, value.shape[-1])

    def by_col(value):
        return value.reshape(cols, col_sides, value.shape[-1])

    def everything(ref, k):
        return ref[k].reshape(groups * sides, ref.shape[-1])

    last = blocks - 1

    def forward_reach(k, g):
        phase = gather_row(forward_ref.at[k - 1, g], g)
        phase.arrived()
        ahead[k, g] += by_col(product(flat(forward_ref[k - 1, g]), factor[k, k - 1], NT))
        scatter_col(ahead.at[k, g], g).start()
        phase.sent()

    def forward_target(k, g):
        phase = scatter_col(ahead.at[k, g], g)
        phase.arrived()
        total = reduced(ahead[k, g, col_me], in_col, g, cols)
        target_row[g, col_me] = right_ref[k, g, col_me] - total
        gather_col(target_row.at[g], g).start()
        phase.sent()

    def forward_multiply(k, g):
        phase = gather_col(target_row.at[g], g)
        phase.arrived()
        part_row[g] = by_row(product(flat(target_row[g]), inverses[k], NT))
        scatter_row(part_row.at[g], g).start()
        phase.sent()

    def forward_solve(k, g):
        phase = scatter_row(part_row.at[g], g)
        phase.arrived()
        forward_ref[k, g, row_me] = reduced(part_row[g, row_me], in_row, g, rows)
        gather_row(forward_ref.at[k, g], g).start()
        phase.sent()

    def forward_rest(k):
        def update(i, _):
            fetch_factor(i, k - 1).wait()
            ahead[i] += product(everything(forward_ref, k - 1), factor[i, k - 1], NT).reshape(ahead.shape[1:])
            return 0

        lax.fori_loop(k + 1, blocks, update, 0)

    def backward_first(g):
        phase = gather_row(forward_ref.at[last, g], g)
        phase.arrived()
        part_col[g] = by_col(product(flat(forward_ref[last, g]), inverses[last], NN))
        scatter_col(part_col.at[g], g).start()
        phase.sent()

    def backward_solve(k, g):
        phase = scatter_col(part_col.at[g], g)
        phase.arrived()
        backward_ref[k, g, col_me] = reduced(part_col[g, col_me], in_col, g, cols)
        gather_col(backward_ref.at[k, g], g).start()
        phase.sent()

    def backward_reach(k, g):
        phase = gather_col(backward_ref.at[k + 1, g], g)
        phase.arrived()
        behind[k, g] += by_row(product(flat(backward_ref[k + 1, g]), factor[k + 1, k], NN))
        scatter_row(behind.at[k, g], g).start()
        phase.sent()

    def backward_target(k, g):
        phase = scatter_row(behind.at[k, g], g)
        phase.arrived()
        total = reduced(behind[k, g, row_me], in_row, g, rows)
        target_col[g, row_me] = forward_ref[k, g, row_me] - total
        gather_row(target_col.at[g], g).start()
        phase.sent()

    def backward_multiply(k, g):
        phase = gather_row(target_col.at[g], g)
        phase.arrived()
        part_col[g] = by_col(product(flat(target_col[g]), inverses[k], NN))
        scatter_col(part_col.at[g], g).start()
        phase.sent()

    def backward_rest(k):
        def update(j, _):
            behind[j] += product(everything(backward_ref, k), factor[k, j], NN).reshape(behind.shape[1:])
            return 0

        lax.fori_loop(0, k - 1, update, 0)

    def late(action, *where):
        for g in range(1, groups):
            action(*where, g)

    fetch_inverse(0).wait()
    for g in range(groups):
        part_row[g] = by_row(product(flat(right_ref[0, g]), inverses[0], NT))
        scatter_row(part_row.at[g], g).start()
    forward_solve(0, 0)
    fetch_factor(1, 0).wait()
    forward_reach(1, 0)

    def forward_half(k):
        forward_target(k, 0)
        late(forward_solve, k - 1)
        late(forward_reach, k)
        forward_rest(k)
        fetch_inverse(k).wait()
        forward_multiply(k, 0)
        late(forward_target, k)
        forward_solve(k, 0)

    def forward_step(k, _):
        forward_half(k)
        fetch_factor(k + 1, k).wait()
        forward_reach(k + 1, 0)
        late(forward_multiply, k)
        return 0

    lax.fori_loop(1, last, forward_step, 0)
    forward_half(last)
    backward_first(0)
    late(forward_multiply, last)

    def backward_half(k):
        backward_reach(k - 1, 0)
        late(backward_solve, k)
        backward_target(k - 1, 0)
        backward_multiply(k - 1, 0)
        late(backward_reach, k - 1)
        backward_rest(k)

    backward_solve(last, 0)
    late(forward_solve, last)
    late(backward_first)
    backward_half(last)

    def backward_step(step, _):
        k = last - step
        backward_solve(k, 0)
        late(backward_target, k)
        late(backward_multiply, k)
        backward_half(k)
        return 0

    lax.fori_loop(1, last, backward_step, 0)
    backward_solve(0, 0)
    late(backward_target, 0)
    late(backward_multiply, 0)
    late(backward_solve, 0)
    for g in range(groups):
        phase = gather_col(backward_ref.at[0, g], g)
        phase.arrived()
        phase.sent()


def local(rows, cols, factor, inverses, right_side):
    blocks, _, row_width, col_width = factor.shape
    sides = right_side.shape[0]
    groups = 2 if sides % (16 * rows) == 0 and sides % (16 * cols) == 0 else 1
    row_sides, col_sides = sides // (groups * rows), sides // (groups * cols)
    wide = (groups, cols, col_sides, row_width)
    narrow = (groups, rows, row_sides, col_width)
    right = right_side.transpose(1, 0, 2).reshape((blocks,) + wide)
    f32 = jnp.float32
    vmem = pl.BlockSpec(memory_space=pltpu.VMEM)
    hbm = pl.BlockSpec(memory_space=pl.ANY)
    dma = pltpu.SemaphoreType.DMA
    forward, backward = pl.pallas_call(
        functools.partial(kernel, rows, cols, groups),
        out_shape=(
            jax.ShapeDtypeStruct((blocks,) + narrow, f32),
            jax.ShapeDtypeStruct((blocks,) + wide, f32),
        ),
        in_specs=[hbm, hbm, vmem],
        out_specs=(vmem, vmem),
        scratch_shapes=[
            pltpu.VMEM(factor.shape, f32),
            pltpu.VMEM(inverses.shape, f32),
            pltpu.VMEM((blocks,) + wide, f32),
            pltpu.VMEM((blocks,) + narrow, f32),
            pltpu.VMEM(wide, f32),
            pltpu.VMEM(narrow, f32),
            pltpu.VMEM(wide, f32),
            pltpu.VMEM(narrow, f32),
            pltpu.VMEM((groups, rows - 1) + narrow[2:], f32),
            pltpu.VMEM((groups, cols - 1) + wide[2:], f32),
            dma((blocks, blocks)),
            dma((blocks,)),
        ] + [dma((groups,))] * 8,
        compiler_params=pltpu.CompilerParams(
            collective_id=0, has_side_effects=True, vmem_limit_bytes=56 * 1024 * 1024
        ),
    )(factor, inverses, right)
    forward = forward.reshape(blocks, sides, col_width).transpose(1, 0, 2)
    backward = backward.reshape(blocks, sides, row_width).transpose(1, 0, 2)
    return forward, backward


def solution(mesh):
    placed = (P(None, None, "row", "col"), P(None, "col", "row"), P(None, None, "row"))
    return jax.shard_map(
        functools.partial(local, mesh.shape["row"], mesh.shape["col"]),
        mesh=mesh,
        in_specs=placed,
        out_specs=(P(None, None, "col"), P(None, None, "row")),
        check_vma=False,
    )
```
